256 devices in a mesh: ctx: 64 (over x, z, core), head: 4 (over y).
Axes of the slice: x: 4, y: 4, z: 8, core: 2. Of those that a mesh axis runs over, the one named last changes fastest.
Arguments:
- queries: bfloat16 [32768, 2048], P('ctx', 'head'), may hold values from -6 to 6
- key_pairs: bfloat16 [32768, 2, 2048], P('ctx', None, 'head'), may hold values from -6 to 6
- value_pairs: bfloat16 [32768, 2, 2048], P('ctx', None, 'head'), may hold values from -6 to 6
- beta_pairs: float32 [32768, 2, 16], P('ctx', None, 'head'), may hold values from 0.2 to 2
- log_decay: float32 [32768, 16], P('ctx', 'head'), may hold values from -0.7 to 0
- query_filter_taps: float32 [4, 2048], P(None, 'head'), may hold values from -3 to 3
- conv_key: float32 [4, 2, 2048], P(None, None, 'head'), may hold values from -3 to 3
- conv_value: float32 [4, 2, 2048], P(None, None, 'head'), may hold values from -3 to 3
- norm_gain: float32 [128], replicated, may hold values from 0.1 to 1.9
- out_weight: bfloat16 [2048, 4096], P(None, 'head'), may hold values from -0.125 to 0.125
Outputs:
- layer_out: bfloat16 [32768, 4096], P('ctx', 'head')
The draws below stay inside these ranges and needn't reach their ends.
All inputs are finite; a program needn't handle non-finite values.
Results may differ from the reference program's by a relative error of at most 0.0055.
Values may be sent and summed in bfloat16 or wider, within the bound.
A program may use at most 128 MiB of HBM per device.

```python
import math
import jax
import jax.numpy as jnp
from jax import lax

HEADS = 16
DK = 128
DV = 128
D = 4096
KERNEL = 4
SPAN = 64
TOK_DEV = 512
STREAM_LENGTH = 32768


def head_classes(key):
    share = 0.5
    return jax.random.uniform(jax.random.fold_in(key, 11), (HEADS,)) < share


def draw_beta_pairs(key, part):
    slow_heads = head_classes(key)
    tensor_dimensions = (STREAM_LENGTH, 2, HEADS)
    fast_values = jax.random.uniform(jax.random.fold_in(key, 21), tensor_dimensions, jnp.float32, 0.2, 1.6)
    gaps = jnp.exp(jax.random.uniform(jax.random.fold_in(key, 22), tensor_dimensions, jnp.float32, math.log(1e-05), math.log(0.0004)))
    return jnp.where(slow_heads[None, None, :], 2.0 - gaps, fast_values)


def draw_log_decay(key, part):
    slow_heads = head_classes(key)
    tensor_dimensions = (STREAM_LENGTH, HEADS)
    widening_ratio = jnp.exp(jax.random.uniform(jax.random.fold_in(key, 31), tensor_dimensions, jnp.float32, math.log(0.5), math.log(2.0)))
    fast_rates = jnp.exp(jax.random.uniform(jax.random.fold_in(key, 32), (HEADS,), jnp.float32, math.log(1.0 / 50.0), math.log(1.0 / 30.0)))
    sudden_clusters = jax.random.randint(jax.random.fold_in(key, 33), tensor_dimensions, 0, STREAM_LENGTH) < 3
    sudden_exponents = jnp.log(jax.random.uniform(jax.random.fold_in(key, 34), tensor_dimensions, jnp.float32, 0.5, 0.8))
    smooth_entries = -(0.4 / STREAM_LENGTH) * widening_ratio + jnp.where(sudden_clusters, sudden_exponents, 0.0)
    fast_values = -fast_rates[None, :] * widening_ratio
    return jnp.where(slow_heads[None, :], smooth_entries, fast_values)


def levels(key, extent, cuts, smallest, high):
    def one(axis_at, parts):
        steps = jax.random.uniform(jax.random.fold_in(jax.random.fold_in(key, 6), axis_at), (parts,), jnp.float32, smallest / len(cuts), high / len(cuts))
        return jnp.repeat(jnp.exp(steps), extent[axis_at] // parts).reshape((-1,) + (1,) * (len(extent) - axis_at - 1))

    gain = one(*cuts[0])
    for cut in cuts[1:]:
        gain = gain * one(*cut)
    return gain


def noise(key, shape, spread, reach, split=(), kind=jnp.bfloat16):
    entries = spread * jax.random.normal(key, shape, jnp.float32)
    if split:
        entries = entries * levels(key, shape, split, -0.22, 0.18)
    return jnp.clip(entries, -reach, reach).astype(kind)


def setup_inputs(seed: int = 0) -> dict:
    key_list = jax.random.split(jax.random.key(seed), 11)
    queries = noise(key_list[0], (STREAM_LENGTH, HEADS * DK), 1.0, 6.0, ((0, 64), (1, 4)))
    key_pairs = noise(key_list[1], (STREAM_LENGTH, 2, HEADS * DK), 1.0, 6.0, ((0, 64), (2, 4)))
    value_pairs = noise(key_list[2], (STREAM_LENGTH, 2, HEADS * DV), 1.0, 6.0, ((0, 64), (2, 4)))
    beta_pairs = draw_beta_pairs(jax.random.fold_in(key_list[10], 71), 0)
    log_decay = draw_log_decay(jax.random.fold_in(key_list[10], 71), 0)
    query_filter_taps = noise(key_list[5], (KERNEL, HEADS * DK), KERNEL ** -0.5, 3.0, ((1, 4),), jnp.float32)
    conv_key = noise(key_list[6], (KERNEL, 2, HEADS * DK), KERNEL ** -0.5, 3.0, ((2, 4),), jnp.float32)
    conv_value = noise(key_list[7], (KERNEL, 2, HEADS * DV), KERNEL ** -0.5, 3.0, ((2, 4),), jnp.float32)
    norm_gain = jnp.clip(1.0 + 0.18 * jax.random.normal(key_list[8], (DV,), jnp.float32), 0.1, 1.9)
    out_weight = noise(key_list[9], (HEADS * DV, D), (HEADS * DV) ** -0.5, 0.125, ((1, 4),))
    return dict(queries=queries, key_pairs=key_pairs, value_pairs=value_pairs, beta_pairs=beta_pairs, log_decay=log_decay, query_filter_taps=query_filter_taps, conv_key=conv_key, conv_value=conv_value, norm_gain=norm_gain, out_weight=out_weight)


PRECISE = lax.Precision.HIGHEST
EPSILON = 1e-06
NORM_EPSILON = 1e-05

def causal_conv(inputs, rim_rows, weights):
    tap_count = weights.shape[0]
    row_count = inputs.shape[0]
    extended = jnp.concatenate([rim_rows, inputs], axis=0)
    summed = jnp.zeros_like(inputs)
    for offset in range(tap_count):
        summed = summed + weights[offset] * extended[offset:offset + row_count]
    return jax.nn.silu(summed)

def unit_rows(vectors):
    return vectors * lax.rsqrt(lax.optimization_barrier(jnp.sum(vectors * vectors, axis=-1, keepdims=True)) + EPSILON)

def span_terms(query_rows, key_rows, value_rows, beta_rows, gammas):
    positions = key_rows.shape[-2]
    query_count = query_rows.shape[-2]
    key_width = key_rows.shape[-1]
    key_inner = jnp.einsum('...id,...jd->...ij', key_rows, key_rows, precision=PRECISE)
    strict_mask = jnp.tril(jnp.ones((positions, positions), jnp.float32), -1)
    system = jnp.eye(positions, dtype=jnp.float32) + strict_mask * beta_rows[..., :, None] * key_inner
    right_sides = jnp.concatenate([beta_rows[..., None] * key_rows, (beta_rows / gammas)[..., None] * value_rows], axis=-1)
    solved = jax.scipy.linalg.solve_triangular(system, right_sides, lower=True, unit_diagonal=True)
    write_keys = solved[..., :key_width]
    write_vals = solved[..., key_width:]
    gamma_query = gammas[..., 1::2]
    visible = jnp.arange(positions)[None, :] <= (2 * jnp.arange(query_count) + 1)[:, None]
    scores = jnp.where(visible, jnp.einsum('...td,...jd->...tj', query_rows, key_rows, precision=PRECISE), 0.0)
    query_hat = gamma_query[..., None] * (query_rows - jnp.einsum('...tj,...jd->...td', scores, write_keys, precision=PRECISE))
    local_out = gamma_query[..., None] * jnp.einsum('...tj,...jv->...tv', scores, write_vals, precision=PRECISE)
    final_gamma = gammas[..., -1][..., None, None]
    transit = final_gamma * (jnp.eye(key_width, dtype=jnp.float32) - jnp.einsum('...jd,...je->...de', write_keys, key_rows, precision=PRECISE))
    inject = final_gamma * jnp.einsum('...jv,...jd->...vd', write_vals, key_rows, precision=PRECISE)
    return (query_hat, local_out, transit, inject)

def prepare(queries, key_pairs, value_pairs, beta_pairs, log_decay, query_filter_taps, conv_key, conv_value, rim_queries, rim_keys, rim_values):
    piece_list = queries.shape[0]
    head_count = beta_pairs.shape[2]
    key_width = queries.shape[1] // head_count
    value_columns = value_pairs.shape[2] // head_count
    span_count = 2 * piece_list // SPAN
    conv_queries = causal_conv(queries.astype(jnp.float32), rim_queries.astype(jnp.float32), query_filter_taps)
    conv_keys = causal_conv(key_pairs.astype(jnp.float32), rim_keys.astype(jnp.float32), conv_key)
    conv_values = causal_conv(value_pairs.astype(jnp.float32), rim_values.astype(jnp.float32), conv_value)
    head_queries = unit_rows(conv_queries.reshape(piece_list, head_count, key_width))
    head_keys = unit_rows(conv_keys.reshape(piece_list, 2, head_count, key_width))
    head_values = conv_values.reshape(piece_list, 2, head_count, value_columns)
    query_blocks = head_queries.transpose(1, 0, 2).reshape(head_count, span_count, SPAN // 2, key_width)
    key_blocks = head_keys.transpose(2, 0, 1, 3).reshape(head_count, span_count, SPAN, key_width)
    value_blocks = head_values.transpose(2, 0, 1, 3).reshape(head_count, span_count, SPAN, value_columns)
    beta_blocks = beta_pairs.transpose(2, 0, 1).reshape(head_count, span_count, SPAN)
    decay_token = log_decay.transpose(1, 0).reshape(head_count, span_count, SPAN // 2)
    decay_steps = jnp.stack([decay_token, jnp.zeros_like(decay_token)], axis=-1).reshape(head_count, span_count, SPAN)
    gammas = jnp.exp(jnp.cumsum(decay_steps, axis=-1))
    return span_terms(query_blocks, key_blocks, value_blocks, beta_blocks, gammas)

def matmul_heads(left, right):
    return jnp.einsum('hij,hjk->hik', left, right, precision=PRECISE)

def chain_outputs(query_hat, local_out, transit, inject, carried):

    def advance(state_now, pieces):
        step_hat, step_local, step_transit, step_inject = pieces
        outputs = jnp.einsum('htd,hvd->htv', step_hat, state_now, precision=PRECISE) + step_local
        return (matmul_heads(state_now, step_transit) + step_inject, outputs)
    moved = tuple((jnp.moveaxis(member, 1, 0) for member in (query_hat, local_out, transit, inject)))
    final_state, outputs = lax.scan(advance, carried, moved)
    return (final_state, jnp.moveaxis(outputs, 0, 1))

def finish(raw_out, norm_gain):
    head_count, span_count, query_count, value_columns = raw_out.shape
    rows_out = raw_out.reshape(head_count, span_count * query_count, value_columns)
    scaled = rows_out * lax.rsqrt(lax.optimization_barrier(jnp.mean(rows_out * rows_out, axis=-1, keepdims=True)) + NORM_EPSILON) * norm_gain
    return scaled.transpose(1, 0, 2).reshape(span_count * query_count, head_count * value_columns).astype(jnp.bfloat16)

def reference(queries, key_pairs, value_pairs, beta_pairs, log_decay, query_filter_taps, conv_key, conv_value, norm_gain, out_weight):
    block_count = STREAM_LENGTH // TOK_DEV
    tap_count = query_filter_taps.shape[0]
    width_query = queries.shape[1]
    width_key = key_pairs.shape[2]
    width_value = value_pairs.shape[2]
    head_count = beta_pairs.shape[2]
    split_queries = queries.reshape(block_count, TOK_DEV, width_query)
    split_keys = key_pairs.reshape(block_count, TOK_DEV, 2, width_key)
    split_values = value_pairs.reshape(block_count, TOK_DEV, 2, width_value)
    split_betas = beta_pairs.reshape(block_count, TOK_DEV, 2, head_count)
    split_decay = log_decay.reshape(block_count, TOK_DEV, head_count)
    start_state = jnp.zeros((head_count, width_value // head_count, width_key // head_count), jnp.float32)
    start_carry = (start_state, jnp.zeros((tap_count - 1, width_query), jnp.bfloat16), jnp.zeros((tap_count - 1, 2, width_key), jnp.bfloat16), jnp.zeros((tap_count - 1, 2, width_value), jnp.bfloat16))
    rim_start = TOK_DEV - (tap_count - 1)

    def block_step(carry, pieces):
        carried, rim_queries, rim_keys, rim_values = carry
        block_queries, block_keys, block_values, block_betas, block_decay = pieces
        query_hat, local_out, transit, inject = prepare(block_queries, block_keys, block_values, block_betas, block_decay, query_filter_taps, conv_key, conv_value, rim_queries, rim_keys, rim_values)
        state_next, raw_out = chain_outputs(query_hat, local_out, transit, inject, carried)
        normed = finish(raw_out, norm_gain)
        block_out = jnp.dot(normed.astype(jnp.float32), out_weight.astype(jnp.float32), preferred_element_type=jnp.float32).astype(jnp.bfloat16)
        new_carry = (state_next, block_queries[rim_start:], block_keys[rim_start:], block_values[rim_start:])
        return (new_carry, block_out)
    final_carry, outputs = lax.scan(block_step, start_carry, (split_queries, split_keys, split_values, split_betas, split_decay))
    return outputs.reshape(STREAM_LENGTH, out_weight.shape[1])
```

```python
import jax
import jax.numpy as jnp
from jax import lax
from jax.sharding import PartitionSpec as P

SPAN = 64


PRECISE = lax.Precision.HIGHEST
EPSILON = 1e-06
NORM_EPSILON = 1e-05


def shifted(value, axis, steps):
    count = lax.axis_size(axis)
    initial, last = (max(0, -steps), min(count, count - steps))
    return lax.ppermute(value, axis, [(source, source + steps) for source in range(initial, last)])


def causal_conv(inputs, rim_rows, weights):
    tap_count = weights.shape[0]
    row_count = inputs.shape[0]
    extended = jnp.concatenate([rim_rows, inputs], axis=0)
    summed = jnp.zeros_like(inputs)
    for offset in range(tap_count):
        summed = summed + weights[offset] * extended[offset : offset + row_count]
    return jax.nn.silu(summed)


def unit_rows(vectors):
    return vectors * lax.rsqrt(jnp.sum(vectors * vectors, axis=-1, keepdims=True) + EPSILON)


def unit_lower_inverse(system):
    positions = system.shape[-1]
    rows = jnp.arange(positions)[:, None]
    cols = jnp.arange(positions)[None, :]
    inverse = jnp.broadcast_to(jnp.eye(positions, dtype=system.dtype), system.shape)
    width = 1
    while width < positions:
        joined = (rows // (2 * width) == cols // (2 * width)) & (rows // width != cols // width)
        coupling = jnp.where(joined & (rows > cols), system, 0.0)
        inverse = inverse - jnp.einsum(
            "...ij,...jk,...kl->...il", inverse, coupling, inverse, precision=PRECISE
        )
        width *= 2
    return inverse


def span_terms(query_rows, key_rows, value_rows, beta_rows, gammas):
    positions = key_rows.shape[-2]
    query_count = query_rows.shape[-2]
    key_width = key_rows.shape[-1]
    key_inner = jnp.einsum("...id,...jd->...ij", key_rows, key_rows, precision=PRECISE)
    strict_mask = jnp.tril(jnp.ones((positions, positions), jnp.float32), -1)
    system = (
        jnp.eye(positions, dtype=jnp.float32) + strict_mask * beta_rows[..., :, None] * key_inner
    )
    right_sides = jnp.concatenate(
        [beta_rows[..., None] * key_rows, (beta_rows / gammas)[..., None] * value_rows], axis=-1
    )
    solved = jnp.einsum(
        "...ij,...jc->...ic", unit_lower_inverse(system), right_sides, precision=PRECISE
    )
    write_keys = solved[..., :key_width]
    write_vals = solved[..., key_width:]
    gamma_query = gammas[..., 1::2]
    visible = jnp.arange(positions)[None, :] <= (2 * jnp.arange(query_count) + 1)[:, None]
    scores = jnp.where(
        visible, jnp.einsum("...td,...jd->...tj", query_rows, key_rows, precision=PRECISE), 0.0
    )
    query_hat = gamma_query[..., None] * (
        query_rows - jnp.einsum("...tj,...jd->...td", scores, write_keys, precision=PRECISE)
    )
    local_out = gamma_query[..., None] * jnp.einsum(
        "...tj,...jv->...tv", scores, write_vals, precision=PRECISE
    )
    final_gamma = gammas[..., -1][..., None, None]
    transit = final_gamma * (
        jnp.eye(key_width, dtype=jnp.float32)
        - jnp.einsum("...jd,...je->...de", write_keys, key_rows, precision=PRECISE)
    )
    inject = final_gamma * jnp.einsum("...jv,...jd->...vd", write_vals, key_rows, precision=PRECISE)
    return (query_hat, local_out, transit, inject)


def prepare(
    queries,
    key_pairs,
    value_pairs,
    beta_pairs,
    log_decay,
    query_filter_taps,
    conv_key,
    conv_value,
    rim_queries,
    rim_keys,
    rim_values,
):
    piece_list = queries.shape[0]
    head_count = beta_pairs.shape[2]
    key_width = queries.shape[1] // head_count
    value_columns = value_pairs.shape[2] // head_count
    span_count = 2 * piece_list // SPAN
    conv_queries = causal_conv(
        queries.astype(jnp.float32), rim_queries.astype(jnp.float32), query_filter_taps
    )
    conv_keys = causal_conv(key_pairs.astype(jnp.float32), rim_keys.astype(jnp.float32), conv_key)
    conv_values = causal_conv(
        value_pairs.astype(jnp.float32), rim_values.astype(jnp.float32), conv_value
    )
    head_queries = unit_rows(conv_queries.reshape(piece_list, head_count, key_width))
    head_keys = unit_rows(conv_keys.reshape(piece_list, 2, head_count, key_width))
    head_values = conv_values.reshape(piece_list, 2, head_count, value_columns)
    query_blocks = head_queries.transpose(1, 0, 2).reshape(
        head_count, span_count, SPAN // 2, key_width
    )
    key_blocks = head_keys.transpose(2, 0, 1, 3).reshape(head_count, span_count, SPAN, key_width)
    value_blocks = head_values.transpose(2, 0, 1, 3).reshape(
        head_count, span_count, SPAN, value_columns
    )
    beta_blocks = beta_pairs.transpose(2, 0, 1).reshape(head_count, span_count, SPAN)
    decay_token = log_decay.transpose(1, 0).reshape(head_count, span_count, SPAN // 2)
    decay_steps = jnp.stack([decay_token, jnp.zeros_like(decay_token)], axis=-1).reshape(
        head_count, span_count, SPAN
    )
    gammas = jnp.exp(jnp.cumsum(decay_steps, axis=-1))
    return span_terms(query_blocks, key_blocks, value_blocks, beta_blocks, gammas)


def matmul_heads(left, right):
    return jnp.einsum("hij,hjk->hik", left, right, precision=PRECISE)


def chain_outputs(query_hat, local_out, transit, inject, carried):

    def advance(state_now, pieces):
        step_hat, step_local, step_transit, step_inject = pieces
        outputs = jnp.einsum("htd,hvd->htv", step_hat, state_now, precision=PRECISE) + step_local
        return (matmul_heads(state_now, step_transit) + step_inject, outputs)

    moved = tuple(
        (jnp.moveaxis(member, 1, 0) for member in (query_hat, local_out, transit, inject))
    )
    final_state, outputs = lax.scan(advance, carried, moved)
    return (final_state, jnp.moveaxis(outputs, 0, 1))


def chain_transforms(transit, inject, identity, zero_state):

    def absorb(carry, pieces):
        product, state_now = carry
        step_transit, step_inject = pieces
        return (
            (
                matmul_heads(product, step_transit),
                matmul_heads(state_now, step_transit) + step_inject,
            ),
            None,
        )

    moved = (jnp.moveaxis(transit, 1, 0), jnp.moveaxis(inject, 1, 0))
    final_maps, unused = lax.scan(absorb, (identity, zero_state), moved)
    return final_maps


def finish(raw_out, norm_gain):
    head_count, span_count, query_count, value_columns = raw_out.shape
    rows_out = raw_out.reshape(head_count, span_count * query_count, value_columns)
    scaled = (
        rows_out
        * lax.rsqrt(jnp.mean(rows_out * rows_out, axis=-1, keepdims=True) + NORM_EPSILON)
        * norm_gain
    )
    return (
        scaled.transpose(1, 0, 2)
        .reshape(span_count * query_count, head_count * value_columns)
        .astype(jnp.bfloat16)
    )


def local(
    queries,
    key_pairs,
    value_pairs,
    beta_pairs,
    log_decay,
    query_filter_taps,
    conv_key,
    conv_value,
    norm_gain,
    out_weight,
):
    piece_list = queries.shape[0]
    rim_start = piece_list - (query_filter_taps.shape[0] - 1)
    rim_queries, rim_keys, rim_values = shifted(
        (queries[rim_start:], key_pairs[rim_start:], value_pairs[rim_start:]), "ctx", 1
    )
    query_hat, local_out, transit, inject = prepare(
        queries,
        key_pairs,
        value_pairs,
        beta_pairs,
        log_decay,
        query_filter_taps,
        conv_key,
        conv_value,
        rim_queries,
        rim_keys,
        rim_values,
    )
    head_count = transit.shape[0]
    key_width = transit.shape[-1]
    value_columns = inject.shape[-2]
    identity = jnp.broadcast_to(
        jnp.eye(key_width, dtype=jnp.float32), (head_count, key_width, key_width)
    )
    zero_state = jnp.zeros((head_count, value_columns, key_width), jnp.float32)
    device_map, device_inject = chain_transforms(transit, inject, identity, zero_state)
    ctx_count = lax.axis_size("ctx")
    ctx_index = lax.axis_index("ctx")
    distance = 1
    while distance < ctx_count:
        if 2 * distance < ctx_count:
            earlier_map, earlier_inject = shifted((device_map, device_inject), "ctx", distance)
            joined_map = matmul_heads(earlier_map, device_map)
        else:
            earlier_inject = shifted(device_inject, "ctx", distance)
            joined_map = device_map
        device_inject = matmul_heads(earlier_inject, device_map) + device_inject
        device_map = jnp.where(ctx_index >= distance, joined_map, device_map)
        distance *= 2
    entering = shifted(device_inject, "ctx", 1)
    final_state, raw_out = chain_outputs(query_hat, local_out, transit, inject, entering)
    normed = finish(raw_out, norm_gain)
    layer_out = jnp.dot(
        lax.all_gather(normed, "head", axis=1, tiled=True),
        out_weight,
        preferred_element_type=jnp.float32,
    )
    return layer_out.astype(jnp.bfloat16)


def solution(mesh):
    return jax.shard_map(
        local,
        mesh=mesh,
        in_specs=(
            P("ctx", "head"),
            P("ctx", None, "head"),
            P("ctx", None, "head"),
            P("ctx", None, "head"),
            P("ctx", "head"),
            P(None, "head"),
            P(None, None, "head"),
            P(None, None, "head"),
            P(),
            P(None, "head"),
        ),
        out_specs=P("ctx", "head"),
        check_vma=False,
    )
```

```python
import jax
import jax.numpy as jnp
from jax import lax
from jax.sharding import PartitionSpec as P

SPAN = 64


PRECISE = lax.Precision.HIGHEST
EPSILON = 1e-06
NORM_EPSILON = 1e-05


def shifted(value, axis, steps):
    count = lax.axis_size(axis)
    initial, last = (max(0, -steps), min(count, count - steps))
    return lax.ppermute(value, axis, [(source, source + steps) for source in range(initial, last)])


def causal_conv(inputs, rim_rows, weights):
    tap_count = weights.shape[0]
    row_count = inputs.shape[0]
    extended = jnp.concatenate([rim_rows, inputs], axis=0)
    summed = jnp.zeros_like(inputs)
    for offset in range(tap_count):
        summed = summed + weights[offset] * extended[offset : offset + row_count]
    return jax.nn.silu(summed)


def unit_rows(vectors):
    return vectors * lax.rsqrt(jnp.sum(vectors * vectors, axis=-1, keepdims=True) + EPSILON)


def unit_lower_inverse(system):
    positions = system.shape[-1]
    rows = jnp.arange(positions)[:, None]
    cols = jnp.arange(positions)[None, :]
    inverse = jnp.broadcast_to(jnp.eye(positions, dtype=system.dtype), system.shape)
    width = 1
    while width < positions:
        joined = (rows // (2 * width) == cols // (2 * width)) & (rows // width != cols // width)
        coupling = jnp.where(joined & (rows > cols), system, 0.0)
        inverse = inverse - jnp.einsum(
            "...ij,...jk,...kl->...il", inverse, coupling, inverse, precision=PRECISE
        )
        width *= 2
    return inverse


def span_terms(query_rows, key_rows, value_rows, beta_rows, gammas):
    positions = key_rows.shape[-2]
    query_count = query_rows.shape[-2]
    key_width = key_rows.shape[-1]
    key_inner = jnp.einsum("...id,...jd->...ij", key_rows, key_rows, precision=PRECISE)
    strict_mask = jnp.tril(jnp.ones((positions, positions), jnp.float32), -1)
    system = (
        jnp.eye(positions, dtype=jnp.float32) + strict_mask * beta_rows[..., :, None] * key_inner
    )
    right_sides = jnp.concatenate(
        [beta_rows[..., None] * key_rows, (beta_rows / gammas)[..., None] * value_rows], axis=-1
    )
    solved = jnp.einsum(
        "...ij,...jc->...ic", unit_lower_inverse(system), right_sides, precision=PRECISE
    )
    write_keys = solved[..., :key_width]
    write_vals = solved[..., key_width:]
    gamma_query = gammas[..., 1::2]
    visible = jnp.arange(positions)[None, :] <= (2 * jnp.arange(query_count) + 1)[:, None]
    scores = jnp.where(
        visible, jnp.einsum("...td,...jd->...tj", query_rows, key_rows, precision=PRECISE), 0.0
    )
    query_hat = gamma_query[..., None] * (
        query_rows - jnp.einsum("...tj,...jd->...td", scores, write_keys, precision=PRECISE)
    )
    local_out = gamma_query[..., None] * jnp.einsum(
        "...tj,...jv->...tv", scores, write_vals, precision=PRECISE
    )
    final_gamma = gammas[..., -1][..., None, None]
    transit = final_gamma * (
        jnp.eye(key_width, dtype=jnp.float32)
        - jnp.einsum("...jd,...je->...de", write_keys, key_rows, precision=PRECISE)
    )
    inject = final_gamma * jnp.einsum("...jv,...jd->...vd", write_vals, key_rows, precision=PRECISE)
    return (query_hat, local_out, transit, inject)


def prepare(
    queries,
    key_pairs,
    value_pairs,
    beta_pairs,
    log_decay,
    query_filter_taps,
    conv_key,
    conv_value,
    rim_queries,
    rim_keys,
    rim_values,
):
    piece_list = queries.shape[0]
    head_count = beta_pairs.shape[2]
    key_width = queries.shape[1] // head_count
    value_columns = value_pairs.shape[2] // head_count
    span_count = 2 * piece_list // SPAN
    conv_queries = causal_conv(
        queries.astype(jnp.float32), rim_queries.astype(jnp.float32), query_filter_taps
    )
    conv_keys = causal_conv(key_pairs.astype(jnp.float32), rim_keys.astype(jnp.float32), conv_key)
    conv_values = causal_conv(
        value_pairs.astype(jnp.float32), rim_values.astype(jnp.float32), conv_value
    )
    head_queries = unit_rows(conv_queries.reshape(piece_list, head_count, key_width))
    head_keys = unit_rows(conv_keys.reshape(piece_list, 2, head_count, key_width))
    head_values = conv_values.reshape(piece_list, 2, head_count, value_columns)
    query_blocks = head_queries.transpose(1, 0, 2).reshape(
        head_count, span_count, SPAN // 2, key_width
    )
    key_blocks = head_keys.transpose(2, 0, 1, 3).reshape(head_count, span_count, SPAN, key_width)
    value_blocks = head_values.transpose(2, 0, 1, 3).reshape(
        head_count, span_count, SPAN, value_columns
    )
    beta_blocks = beta_pairs.transpose(2, 0, 1).reshape(head_count, span_count, SPAN)
    decay_token = log_decay.transpose(1, 0).reshape(head_count, span_count, SPAN // 2)
    decay_steps = jnp.stack([decay_token, jnp.zeros_like(decay_token)], axis=-1).reshape(
        head_count, span_count, SPAN
    )
    gammas = jnp.exp(jnp.cumsum(decay_steps, axis=-1))
    return span_terms(query_blocks, key_blocks, value_blocks, beta_blocks, gammas)


def matmul_heads(left, right):
    return jnp.einsum("hij,hjk->hik", left, right, precision=PRECISE)


def chain_outputs(query_hat, local_out, transit, inject, carried):

    def advance(state_now, pieces):
        step_hat, step_local, step_transit, step_inject = pieces
        outputs = jnp.einsum("htd,hvd->htv", step_hat, state_now, precision=PRECISE) + step_local
        return (matmul_heads(state_now, step_transit) + step_inject, outputs)

    moved = tuple(
        (jnp.moveaxis(member, 1, 0) for member in (query_hat, local_out, transit, inject))
    )
    final_state, outputs = lax.scan(advance, carried, moved)
    return (final_state, jnp.moveaxis(outputs, 0, 1))


def chain_transforms(transit, inject, identity, zero_state):

    def absorb(carry, pieces):
        product, state_now = carry
        step_transit, step_inject = pieces
        return (
            (
                matmul_heads(product, step_transit),
                matmul_heads(state_now, step_transit) + step_inject,
            ),
            carry,
        )

    moved = (jnp.moveaxis(transit, 1, 0), jnp.moveaxis(inject, 1, 0))
    return lax.scan(absorb, (identity, zero_state), moved)


def finish(raw_out, norm_gain):
    head_count, span_count, query_count, value_columns = raw_out.shape
    rows_out = raw_out.reshape(head_count, span_count * query_count, value_columns)
    scaled = (
        rows_out
        * lax.rsqrt(jnp.mean(rows_out * rows_out, axis=-1, keepdims=True) + NORM_EPSILON)
        * norm_gain
    )
    return (
        scaled.transpose(1, 0, 2)
        .reshape(span_count * query_count, head_count * value_columns)
        .astype(jnp.bfloat16)
    )


def local(
    queries,
    key_pairs,
    value_pairs,
    beta_pairs,
    log_decay,
    query_filter_taps,
    conv_key,
    conv_value,
    norm_gain,
    out_weight,
):
    piece_list = queries.shape[0]
    rim_start = piece_list - (query_filter_taps.shape[0] - 1)
    rim_queries, rim_keys, rim_values = shifted(
        (queries[rim_start:], key_pairs[rim_start:], value_pairs[rim_start:]), "ctx", 1
    )
    query_hat, local_out, transit, inject = prepare(
        queries,
        key_pairs,
        value_pairs,
        beta_pairs,
        log_decay,
        query_filter_taps,
        conv_key,
        conv_value,
        rim_queries,
        rim_keys,
        rim_values,
    )
    head_count = transit.shape[0]
    key_width = transit.shape[-1]
    value_columns = inject.shape[-2]
    identity = jnp.broadcast_to(
        jnp.eye(key_width, dtype=jnp.float32), (head_count, key_width, key_width)
    )
    zero_state = jnp.zeros((head_count, value_columns, key_width), jnp.float32)
    (device_map, device_inject), (chunk_maps, chunk_injects) = chain_transforms(
        transit, inject, identity, zero_state
    )
    mapped_queries = jnp.einsum("hctd,ched->hcte", query_hat, chunk_maps, precision=PRECISE)
    known_out = local_out + jnp.einsum(
        "hctd,chvd->hctv", query_hat, chunk_injects, precision=PRECISE
    )
    ctx_count = lax.axis_size("ctx")
    ctx_index = lax.axis_index("ctx")
    width = 1
    while 2 * width < ctx_count - 1:
        earlier_map, earlier_inject = shifted((device_map, device_inject), "ctx", width)
        device_inject = matmul_heads(earlier_inject, device_map) + device_inject
        device_map = jnp.where(
            ctx_index >= width, matmul_heads(earlier_map, device_map), device_map
        )
        width *= 2
    near_map, near_inject = shifted((device_map, device_inject), "ctx", 1)
    far_inject = shifted(device_inject, "ctx", width + 1)
    entering = matmul_heads(far_inject, near_map) + near_inject
    raw_out = known_out + jnp.einsum("hcte,hve->hctv", mapped_queries, entering, precision=PRECISE)
    normed = finish(raw_out, norm_gain)
    head_devices = lax.axis_size("head")
    head_index = lax.axis_index("head")
    group_width = normed.shape[1]
    layer_out = None
    for step in range(head_devices):
        if step == 0:
            group_rows = normed
        else:
            group_rows = lax.ppermute(
                normed, "head", [(source, (source + step) % head_devices) for source in range(head_devices)]
            )
        group_weight = lax.dynamic_slice_in_dim(
            out_weight, ((head_index - step) % head_devices) * group_width, group_width, axis=0
        )
        part = jnp.dot(group_rows, group_weight, preferred_element_type=jnp.float32)
        layer_out = part if layer_out is None else layer_out + part
    return layer_out.astype(jnp.bfloat16)


def solution(mesh):
    return jax.shard_map(
        local,
        mesh=mesh,
        in_specs=(
            P("ctx", "head"),
            P("ctx", None, "head"),
            P("ctx", None, "head"),
            P("ctx", None, "head"),
            P("ctx", "head"),
            P(None, "head"),
            P(None, None, "head"),
            P(None, None, "head"),
            P(),
            P(None, "head"),
        ),
        out_specs=P("ctx", "head"),
        check_vma=False,
    )
```

```python
import jax
import jax.numpy as jnp
from jax import lax
from jax.sharding import PartitionSpec as P

SPAN = 64


PRECISE = lax.Precision.HIGHEST
EPSILON = 1e-06
NORM_EPSILON = 1e-05


def shifted(value, axis, steps):
    count = lax.axis_size(axis)
    initial, last = (max(0, -steps), min(count, count - steps))
    return lax.ppermute(value, axis, [(source, source + steps) for source in range(initial, last)])


def causal_conv(inputs, rim_rows, weights):
    tap_count = weights.shape[0]
    row_count = inputs.shape[0]
    extended = jnp.concatenate([rim_rows, inputs], axis=0)
    summed = jnp.zeros_like(inputs)
    for offset in range(tap_count):
        summed = summed + weights[offset] * extended[offset : offset + row_count]
    return jax.nn.silu(summed)


def unit_rows(vectors):
    return vectors * lax.rsqrt(jnp.sum(vectors * vectors, axis=-1, keepdims=True) + EPSILON)


def unit_lower_inverse(system):
    positions = system.shape[-1]
    rows = jnp.arange(positions)[:, None]
    cols = jnp.arange(positions)[None, :]
    inverse = jnp.broadcast_to(jnp.eye(positions, dtype=system.dtype), system.shape)
    width = 1
    while width < positions:
        joined = (rows // (2 * width) == cols // (2 * width)) & (rows // width != cols // width)
        coupling = jnp.where(joined & (rows > cols), system, 0.0)
        inverse = inverse - jnp.einsum(
            "...ij,...jk,...kl->...il", inverse, coupling, inverse, precision=PRECISE
        )
        width *= 2
    return inverse


def span_terms(query_rows, key_rows, value_rows, beta_rows, gammas):
    positions = key_rows.shape[-2]
    query_count = query_rows.shape[-2]
    key_width = key_rows.shape[-1]
    key_inner = jnp.einsum("...id,...jd->...ij", key_rows, key_rows, precision=PRECISE)
    strict_mask = jnp.tril(jnp.ones((positions, positions), jnp.float32), -1)
    system = (
        jnp.eye(positions, dtype=jnp.float32) + strict_mask * beta_rows[..., :, None] * key_inner
    )
    right_sides = jnp.concatenate(
        [beta_rows[..., None] * key_rows, (beta_rows / gammas)[..., None] * value_rows], axis=-1
    )
    solved = jnp.einsum(
        "...ij,...jc->...ic", unit_lower_inverse(system), right_sides, precision=PRECISE
    )
    write_keys = solved[..., :key_width]
    write_vals = solved[..., key_width:]
    gamma_query = gammas[..., 1::2]
    visible = jnp.arange(positions)[None, :] <= (2 * jnp.arange(query_count) + 1)[:, None]
    scores = jnp.where(
        visible, jnp.einsum("...td,...jd->...tj", query_rows, key_rows, precision=PRECISE), 0.0
    )
    query_hat = gamma_query[..., None] * (
        query_rows - jnp.einsum("...tj,...jd->...td", scores, write_keys, precision=PRECISE)
    )
    local_out = gamma_query[..., None] * jnp.einsum(
        "...tj,...jv->...tv", scores, write_vals, precision=PRECISE
    )
    final_gamma = gammas[..., -1][..., None, None]
    transit = final_gamma * (
        jnp.eye(key_width, dtype=jnp.float32)
        - jnp.einsum("...jd,...je->...de", write_keys, key_rows, precision=PRECISE)
    )
    inject = final_gamma * jnp.einsum("...jv,...jd->...vd", write_vals, key_rows, precision=PRECISE)
    return (query_hat, local_out, transit, inject)


def prepare(
    queries,
    key_pairs,
    value_pairs,
    beta_pairs,
    log_decay,
    query_filter_taps,
    conv_key,
    conv_value,
    rim_queries,
    rim_keys,
    rim_values,
):
    piece_list = queries.shape[0]
    head_count = beta_pairs.shape[2]
    key_width = queries.shape[1] // head_count
    value_columns = value_pairs.shape[2] // head_count
    span_count = 2 * piece_list // SPAN
    conv_queries = causal_conv(
        queries.astype(jnp.float32), rim_queries.astype(jnp.float32), query_filter_taps
    )
    conv_keys = causal_conv(key_pairs.astype(jnp.float32), rim_keys.astype(jnp.float32), conv_key)
    conv_values = causal_conv(
        value_pairs.astype(jnp.float32), rim_values.astype(jnp.float32), conv_value
    )
    head_queries = unit_rows(conv_queries.reshape(piece_list, head_count, key_width))
    head_keys = unit_rows(conv_keys.reshape(piece_list, 2, head_count, key_width))
    head_values = conv_values.reshape(piece_list, 2, head_count, value_columns)
    query_blocks = head_queries.transpose(1, 0, 2).reshape(
        head_count, span_count, SPAN // 2, key_width
    )
    key_blocks = head_keys.transpose(2, 0, 1, 3).reshape(head_count, span_count, SPAN, key_width)
    value_blocks = head_values.transpose(2, 0, 1, 3).reshape(
        head_count, span_count, SPAN, value_columns
    )
    beta_blocks = beta_pairs.transpose(2, 0, 1).reshape(head_count, span_count, SPAN)
    decay_token = log_decay.transpose(1, 0).reshape(head_count, span_count, SPAN // 2)
    decay_steps = jnp.stack([decay_token, jnp.zeros_like(decay_token)], axis=-1).reshape(
        head_count, span_count, SPAN
    )
    gammas = jnp.exp(jnp.cumsum(decay_steps, axis=-1))
    return span_terms(query_blocks, key_blocks, value_blocks, beta_blocks, gammas)


def matmul_heads(left, right):
    return jnp.einsum("hij,hjk->hik", left, right, precision=PRECISE)


def chunk_prefixes(transit, inject):
    head_count, chunk_count, key_width = transit.shape[:3]
    value_columns = inject.shape[2]
    maps, injects = transit, inject
    shift = 1
    while shift < chunk_count:
        earlier_maps = jnp.concatenate(
            [
                jnp.broadcast_to(
                    jnp.eye(key_width, dtype=maps.dtype), (head_count, shift, key_width, key_width)
                ),
                maps[:, :-shift],
            ],
            axis=1,
        )
        earlier_injects = jnp.concatenate(
            [
                jnp.zeros((head_count, shift, value_columns, key_width), injects.dtype),
                injects[:, :-shift],
            ],
            axis=1,
        )
        injects = (
            jnp.einsum("hcvk,hckl->hcvl", earlier_injects, maps, precision=PRECISE) + injects
        )
        maps = jnp.einsum("hcjk,hckl->hcjl", earlier_maps, maps, precision=PRECISE)
        shift *= 2
    chunk_maps = jnp.concatenate(
        [
            jnp.broadcast_to(jnp.eye(key_width, dtype=maps.dtype), (head_count, 1, key_width, key_width)),
            maps[:, :-1],
        ],
        axis=1,
    )
    chunk_injects = jnp.concatenate(
        [jnp.zeros((head_count, 1, value_columns, key_width), injects.dtype), injects[:, :-1]],
        axis=1,
    )
    return (maps[:, -1], injects[:, -1]), (chunk_maps, chunk_injects)


def finish(raw_out, norm_gain):
    head_count, span_count, query_count, value_columns = raw_out.shape
    rows_out = raw_out.reshape(head_count, span_count * query_count, value_columns)
    scaled = (
        rows_out
        * lax.rsqrt(jnp.mean(rows_out * rows_out, axis=-1, keepdims=True) + NORM_EPSILON)
        * norm_gain
    )
    return (
        scaled.transpose(1, 0, 2)
        .reshape(span_count * query_count, head_count * value_columns)
        .astype(jnp.bfloat16)
    )


def local(
    queries,
    key_pairs,
    value_pairs,
    beta_pairs,
    log_decay,
    query_filter_taps,
    conv_key,
    conv_value,
    norm_gain,
    out_weight,
):
    piece_list = queries.shape[0]
    rim_start = piece_list - (query_filter_taps.shape[0] - 1)
    rim_queries, rim_keys, rim_values = shifted(
        (queries[rim_start:], key_pairs[rim_start:], value_pairs[rim_start:]), "ctx", 1
    )
    query_hat, local_out, transit, inject = prepare(
        queries,
        key_pairs,
        value_pairs,
        beta_pairs,
        log_decay,
        query_filter_taps,
        conv_key,
        conv_value,
        rim_queries,
        rim_keys,
        rim_values,
    )
    head_count = transit.shape[0]
    key_width = transit.shape[-1]
    value_columns = inject.shape[-2]
    (device_map, device_inject), (chunk_maps, chunk_injects) = chunk_prefixes(transit, inject)
    mapped_queries = jnp.einsum("hctd,hced->hcte", query_hat, chunk_maps, precision=PRECISE)
    known_out = local_out + jnp.einsum(
        "hctd,hcvd->hctv", query_hat, chunk_injects, precision=PRECISE
    )
    ctx_count = lax.axis_size("ctx")
    ctx_index = lax.axis_index("ctx")
    width = 1
    while 2 * width < ctx_count - 1:
        earlier_map, earlier_inject = shifted((device_map, device_inject), "ctx", width)
        device_inject = matmul_heads(earlier_inject, device_map) + device_inject
        device_map = jnp.where(
            ctx_index >= width, matmul_heads(earlier_map, device_map), device_map
        )
        width *= 2
    near_map, near_inject = shifted((device_map, device_inject), "ctx", 1)
    far_inject = shifted(device_inject, "ctx", width + 1)
    entering = matmul_heads(far_inject, near_map) + near_inject
    raw_out = known_out + jnp.einsum("hcte,hve->hctv", mapped_queries, entering, precision=PRECISE)
    normed = finish(raw_out, norm_gain)
    head_devices = lax.axis_size("head")
    head_index = lax.axis_index("head")
    group_width = normed.shape[1]
    layer_out = None
    for step in range(head_devices):
        if step == 0:
            group_rows = normed
        else:
            group_rows = lax.ppermute(
                normed, "head", [(source, (source + step) % head_devices) for source in range(head_devices)]
            )
        group_weight = lax.dynamic_slice_in_dim(
            out_weight, ((head_index - step) % head_devices) * group_width, group_width, axis=0
        )
        part = jnp.dot(group_rows, group_weight, preferred_element_type=jnp.float32)
        layer_out = part if layer_out is None else layer_out + part
    return layer_out.astype(jnp.bfloat16)


def solution(mesh):
    return jax.shard_map(
        local,
        mesh=mesh,
        in_specs=(
            P("ctx", "head"),
            P("ctx", None, "head"),
            P("ctx", None, "head"),
            P("ctx", None, "head"),
            P("ctx", "head"),
            P(None, "head"),
            P(None, None, "head"),
            P(None, None, "head"),
            P(),
            P(None, "head"),
        ),
        out_specs=P("ctx", "head"),
        check_vma=False,
    )
```

```python
import jax
import jax.numpy as jnp
from jax import lax
from jax.sharding import PartitionSpec as P

SPAN = 64


PRECISE = lax.Precision.HIGHEST
EPSILON = 1e-06
NORM_EPSILON = 1e-05


def shifted(value, axis, steps):
    count = lax.axis_size(axis)
    initial, last = (max(0, -steps), min(count, count - steps))
    return lax.ppermute(value, axis, [(source, source + steps) for source in range(initial, last)])


def causal_conv(inputs, rim_rows, weights):
    tap_count = weights.shape[0]
    row_count = inputs.shape[0]
    extended = jnp.concatenate([rim_rows, inputs], axis=0)
    summed = jnp.zeros_like(inputs)
    for offset in range(tap_count):
        summed = summed + weights[offset] * extended[offset : offset + row_count]
    return jax.nn.silu(summed)


def unit_rows(vectors):
    return vectors * lax.rsqrt(jnp.sum(vectors * vectors, axis=-1, keepdims=True) + EPSILON)


def unit_lower_inverse(system):
    positions = system.shape[-1]
    rows = jnp.arange(positions)[:, None]
    cols = jnp.arange(positions)[None, :]
    inverse = jnp.broadcast_to(jnp.eye(positions, dtype=system.dtype), system.shape)
    width = 1
    while width < positions:
        joined = (rows // (2 * width) == cols // (2 * width)) & (rows // width != cols // width)
        coupling = jnp.where(joined & (rows > cols), system, 0.0)
        inverse = inverse - jnp.einsum(
            "...ij,...jk,...kl->...il", inverse, coupling, inverse, precision=PRECISE
        )
        width *= 2
    return inverse


def span_terms(query_rows, key_rows, value_rows, beta_rows, gammas):
    positions = key_rows.shape[-2]
    query_count = query_rows.shape[-2]
    key_width = key_rows.shape[-1]
    key_inner = jnp.einsum("...id,...jd->...ij", key_rows, key_rows, precision=PRECISE)
    strict_mask = jnp.tril(jnp.ones((positions, positions), jnp.float32), -1)
    system = (
        jnp.eye(positions, dtype=jnp.float32) + strict_mask * beta_rows[..., :, None] * key_inner
    )
    right_sides = jnp.concatenate(
        [beta_rows[..., None] * key_rows, (beta_rows / gammas)[..., None] * value_rows], axis=-1
    )
    solved = jnp.einsum(
        "...ij,...jc->...ic", unit_lower_inverse(system), right_sides, precision=PRECISE
    )
    write_keys = solved[..., :key_width]
    write_vals = solved[..., key_width:]
    gamma_query = gammas[..., 1::2]
    visible = jnp.arange(positions)[None, :] <= (2 * jnp.arange(query_count) + 1)[:, None]
    scores = jnp.where(
        visible, jnp.einsum("...td,...jd->...tj", query_rows, key_rows, precision=PRECISE), 0.0
    )
    query_hat = gamma_query[..., None] * (
        query_rows - jnp.einsum("...tj,...jd->...td", scores, write_keys, precision=PRECISE)
    )
    local_out = gamma_query[..., None] * jnp.einsum(
        "...tj,...jv->...tv", scores, write_vals, precision=PRECISE
    )
    final_gamma = gammas[..., -1][..., None, None]
    transit = final_gamma * (
        jnp.eye(key_width, dtype=jnp.float32)
        - jnp.einsum("...jd,...je->...de", write_keys, key_rows, precision=PRECISE)
    )
    inject = final_gamma * jnp.einsum("...jv,...jd->...vd", write_vals, key_rows, precision=PRECISE)
    return (query_hat, local_out, transit, inject)


def prepare(
    queries,
    key_pairs,
    value_pairs,
    beta_pairs,
    log_decay,
    query_filter_taps,
    conv_key,
    conv_value,
    rim_queries,
    rim_keys,
    rim_values,
):
    piece_list = queries.shape[0]
    head_count = beta_pairs.shape[2]
    key_width = queries.shape[1] // head_count
    value_columns = value_pairs.shape[2] // head_count
    span_count = 2 * piece_list // SPAN
    conv_queries = causal_conv(
        queries.astype(jnp.float32), rim_queries.astype(jnp.float32), query_filter_taps
    )
    conv_keys = causal_conv(key_pairs.astype(jnp.float32), rim_keys.astype(jnp.float32), conv_key)
    conv_values = causal_conv(
        value_pairs.astype(jnp.float32), rim_values.astype(jnp.float32), conv_value
    )
    head_queries = unit_rows(conv_queries.reshape(piece_list, head_count, key_width))
    head_keys = unit_rows(conv_keys.reshape(piece_list, 2, head_count, key_width))
    head_values = conv_values.reshape(piece_list, 2, head_count, value_columns)
    query_blocks = head_queries.transpose(1, 0, 2).reshape(
        head_count, span_count, SPAN // 2, key_width
    )
    key_blocks = head_keys.transpose(2, 0, 1, 3).reshape(head_count, span_count, SPAN, key_width)
    value_blocks = head_values.transpose(2, 0, 1, 3).reshape(
        head_count, span_count, SPAN, value_columns
    )
    beta_blocks = beta_pairs.transpose(2, 0, 1).reshape(head_count, span_count, SPAN)
    decay_token = log_decay.transpose(1, 0).reshape(head_count, span_count, SPAN // 2)
    decay_steps = jnp.stack([decay_token, jnp.zeros_like(decay_token)], axis=-1).reshape(
        head_count, span_count, SPAN
    )
    gammas = jnp.exp(jnp.cumsum(decay_steps, axis=-1))
    return span_terms(query_blocks, key_blocks, value_blocks, beta_blocks, gammas)


def matmul_heads(left, right):
    return jnp.einsum("hij,hjk->hik", left, right, precision=PRECISE)


def chunk_prefixes(transit, inject):
    head_count, chunk_count, key_width = transit.shape[:3]
    value_columns = inject.shape[2]
    maps, injects = transit, inject
    shift = 1
    while shift < chunk_count:
        earlier_maps = jnp.concatenate(
            [
                jnp.broadcast_to(
                    jnp.eye(key_width, dtype=maps.dtype), (head_count, shift, key_width, key_width)
                ),
                maps[:, :-shift],
            ],
            axis=1,
        )
        earlier_injects = jnp.concatenate(
            [
                jnp.zeros((head_count, shift, value_columns, key_width), injects.dtype),
                injects[:, :-shift],
            ],
            axis=1,
        )
        injects = (
            jnp.einsum("hcvk,hckl->hcvl", earlier_injects, maps, precision=PRECISE) + injects
        )
        maps = jnp.einsum("hcjk,hckl->hcjl", earlier_maps, maps, precision=PRECISE)
        shift *= 2
    chunk_maps = jnp.concatenate(
        [
            jnp.broadcast_to(jnp.eye(key_width, dtype=maps.dtype), (head_count, 1, key_width, key_width)),
            maps[:, :-1],
        ],
        axis=1,
    )
    chunk_injects = jnp.concatenate(
        [jnp.zeros((head_count, 1, value_columns, key_width), injects.dtype), injects[:, :-1]],
        axis=1,
    )
    return (maps[:, -1], injects[:, -1]), (chunk_maps, chunk_injects)


def finish(raw_out, norm_gain):
    head_count, span_count, query_count, value_columns = raw_out.shape
    rows_out = raw_out.reshape(head_count, span_count * query_count, value_columns)
    scaled = (
        rows_out
        * lax.rsqrt(jnp.mean(rows_out * rows_out, axis=-1, keepdims=True) + NORM_EPSILON)
        * norm_gain
    )
    return (
        scaled.transpose(1, 0, 2)
        .reshape(span_count * query_count, head_count * value_columns)
        .astype(jnp.bfloat16)
    )


def local(
    queries,
    key_pairs,
    value_pairs,
    beta_pairs,
    log_decay,
    query_filter_taps,
    conv_key,
    conv_value,
    norm_gain,
    out_weight,
):
    piece_list = queries.shape[0]
    rim_start = piece_list - (query_filter_taps.shape[0] - 1)
    rim_queries, rim_keys, rim_values = shifted(
        (queries[rim_start:], key_pairs[rim_start:], value_pairs[rim_start:]), "ctx", 1
    )
    query_hat, local_out, transit, inject = prepare(
        queries,
        key_pairs,
        value_pairs,
        beta_pairs,
        log_decay,
        query_filter_taps,
        conv_key,
        conv_value,
        rim_queries,
        rim_keys,
        rim_values,
    )
    head_count = transit.shape[0]
    key_width = transit.shape[-1]
    value_columns = inject.shape[-2]
    (device_map, device_inject), (chunk_maps, chunk_injects) = chunk_prefixes(transit, inject)
    mapped_queries = jnp.einsum("hctd,hced->hcte", query_hat, chunk_maps, precision=PRECISE)
    known_out = local_out + jnp.einsum(
        "hctd,hcvd->hctv", query_hat, chunk_injects, precision=PRECISE
    )
    ctx_count = lax.axis_size("ctx")
    ctx_index = lax.axis_index("ctx")
    identity = jnp.eye(device_map.shape[-1], dtype=device_map.dtype)
    radix = 4
    width = 1
    while radix * width < ctx_count - 1:
        earlier = []
        for multiple in range(1, radix):
            if multiple * width < ctx_count:
                earlier_map, earlier_inject = shifted(
                    (device_map, device_inject), "ctx", multiple * width
                )
                earlier_map = jnp.where(ctx_index >= multiple * width, earlier_map, identity)
                earlier.append((earlier_map, earlier_inject))
        joined_inject = earlier[-1][1]
        joined_map = earlier[-1][0]
        for earlier_map, earlier_inject in earlier[-2::-1]:
            joined_inject = matmul_heads(joined_inject, earlier_map) + earlier_inject
            joined_map = matmul_heads(joined_map, earlier_map)
        device_inject = matmul_heads(joined_inject, device_map) + device_inject
        device_map = matmul_heads(joined_map, device_map)
        width *= radix
    pieces = []
    offset = 1
    while offset < ctx_count:
        if offset + width < ctx_count:
            pieces.append(shifted((device_map, device_inject), "ctx", offset))
        else:
            pieces.append((None, shifted(device_inject, "ctx", offset)))
        offset += width
    entering = pieces[-1][1]
    for piece_map, piece_inject in pieces[-2::-1]:
        entering = matmul_heads(entering, piece_map) + piece_inject
    raw_out = known_out + jnp.einsum("hcte,hve->hctv", mapped_queries, entering, precision=PRECISE)
    normed = finish(raw_out, norm_gain)
    head_devices = lax.axis_size("head")
    head_index = lax.axis_index("head")
    group_width = normed.shape[1]
    layer_out = None
    for step in range(head_devices):
        if step == 0:
            group_rows = normed
        else:
            group_rows = lax.ppermute(
                normed, "head", [(source, (source + step) % head_devices) for source in range(head_devices)]
            )
        group_weight = lax.dynamic_slice_in_dim(
            out_weight, ((head_index - step) % head_devices) * group_width, group_width, axis=0
        )
        part = jnp.dot(group_rows, group_weight, preferred_element_type=jnp.float32)
        layer_out = part if layer_out is None else layer_out + part
    return layer_out.astype(jnp.bfloat16)


def solution(mesh):
    return jax.shard_map(
        local,
        mesh=mesh,
        in_specs=(
            P("ctx", "head"),
            P("ctx", None, "head"),
            P("ctx", None, "head"),
            P("ctx", None, "head"),
            P("ctx", "head"),
            P(None, "head"),
            P(None, None, "head"),
            P(None, None, "head"),
            P(),
            P(None, "head"),
        ),
        out_specs=P("ctx", "head"),
        check_vma=False,
    )
```

```python
import jax
import jax.numpy as jnp
from jax import lax
from jax.sharding import PartitionSpec as P

SPAN = 64


PRECISE = lax.Precision.HIGHEST
EPSILON = 1e-06
NORM_EPSILON = 1e-05


def shifted(value, axis, steps):
    count = lax.axis_size(axis)
    initial, last = (max(0, -steps), min(count, count - steps))
    return lax.ppermute(value, axis, [(source, source + steps) for source in range(initial, last)])


def causal_conv(inputs, rim_rows, weights):
    tap_count = weights.shape[0]
    row_count = inputs.shape[0]
    extended = jnp.concatenate([rim_rows, inputs], axis=0)
    summed = jnp.zeros_like(inputs)
    for offset in range(tap_count):
        summed = summed + weights[offset] * extended[offset : offset + row_count]
    return jax.nn.silu(summed)


def unit_rows(vectors):
    return vectors * lax.rsqrt(jnp.sum(vectors * vectors, axis=-1, keepdims=True) + EPSILON)


def unit_lower_inverse(system):
    positions = system.shape[-1]
    rows = jnp.arange(positions)[:, None]
    cols = jnp.arange(positions)[None, :]
    inverse = jnp.broadcast_to(jnp.eye(positions, dtype=system.dtype), system.shape)
    width = 1
    while width < positions:
        joined = (rows // (2 * width) == cols // (2 * width)) & (rows // width != cols // width)
        coupling = jnp.where(joined & (rows > cols), system, 0.0)
        inverse = inverse - jnp.einsum(
            "...ij,...jk,...kl->...il", inverse, coupling, inverse, precision=PRECISE
        )
        width *= 2
    return inverse


def span_terms(query_rows, key_rows, value_rows, beta_rows, gammas):
    positions = key_rows.shape[-2]
    query_count = query_rows.shape[-2]
    key_width = key_rows.shape[-1]
    key_inner = jnp.einsum("...id,...jd->...ij", key_rows, key_rows, precision=PRECISE)
    strict_mask = jnp.tril(jnp.ones((positions, positions), jnp.float32), -1)
    system = (
        jnp.eye(positions, dtype=jnp.float32) + strict_mask * beta_rows[..., :, None] * key_inner
    )
    right_sides = jnp.concatenate(
        [beta_rows[..., None] * key_rows, (beta_rows / gammas)[..., None] * value_rows], axis=-1
    )
    solved = jnp.einsum(
        "...ij,...jc->...ic", unit_lower_inverse(system), right_sides, precision=PRECISE
    )
    write_keys = solved[..., :key_width]
    write_vals = solved[..., key_width:]
    gamma_query = gammas[..., 1::2]
    visible = jnp.arange(positions)[None, :] <= (2 * jnp.arange(query_count) + 1)[:, None]
    scores = jnp.where(
        visible, jnp.einsum("...td,...jd->...tj", query_rows, key_rows, precision=PRECISE), 0.0
    )
    query_hat = gamma_query[..., None] * (
        query_rows - jnp.einsum("...tj,...jd->...td", scores, write_keys, precision=PRECISE)
    )
    local_out = gamma_query[..., None] * jnp.einsum(
        "...tj,...jv->...tv", scores, write_vals, precision=PRECISE
    )
    final_gamma = gammas[..., -1][..., None, None]
    transit = final_gamma * (
        jnp.eye(key_width, dtype=jnp.float32)
        - jnp.einsum("...jd,...je->...de", write_keys, key_rows, precision=PRECISE)
    )
    inject = final_gamma * jnp.einsum("...jv,...jd->...vd", write_vals, key_rows, precision=PRECISE)
    return (query_hat, local_out, transit, inject)


def prepare(
    queries,
    key_pairs,
    value_pairs,
    beta_pairs,
    log_decay,
    query_filter_taps,
    conv_key,
    conv_value,
    rim_queries,
    rim_keys,
    rim_values,
):
    piece_list = queries.shape[0]
    head_count = beta_pairs.shape[2]
    key_width = queries.shape[1] // head_count
    value_columns = value_pairs.shape[2] // head_count
    span_count = 2 * piece_list // SPAN
    conv_queries = causal_conv(
        queries.astype(jnp.float32), rim_queries.astype(jnp.float32), query_filter_taps
    )
    conv_keys = causal_conv(key_pairs.astype(jnp.float32), rim_keys.astype(jnp.float32), conv_key)
    conv_values = causal_conv(
        value_pairs.astype(jnp.float32), rim_values.astype(jnp.float32), conv_value
    )
    head_queries = unit_rows(conv_queries.reshape(piece_list, head_count, key_width))
    head_keys = unit_rows(conv_keys.reshape(piece_list, 2, head_count, key_width))
    head_values = conv_values.reshape(piece_list, 2, head_count, value_columns)
    query_blocks = head_queries.transpose(1, 0, 2).reshape(
        head_count, span_count, SPAN // 2, key_width
    )
    key_blocks = head_keys.transpose(2, 0, 1, 3).reshape(head_count, span_count, SPAN, key_width)
    value_blocks = head_values.transpose(2, 0, 1, 3).reshape(
        head_count, span_count, SPAN, value_columns
    )
    beta_blocks = beta_pairs.transpose(2, 0, 1).reshape(head_count, span_count, SPAN)
    decay_token = log_decay.transpose(1, 0).reshape(head_count, span_count, SPAN // 2)
    decay_steps = jnp.stack([decay_token, jnp.zeros_like(decay_token)], axis=-1).reshape(
        head_count, span_count, SPAN
    )
    gammas = jnp.exp(jnp.cumsum(decay_steps, axis=-1))
    return span_terms(query_blocks, key_blocks, value_blocks, beta_blocks, gammas)


def matmul_heads(left, right):
    return jnp.einsum("hij,hjk->hik", left, right, precision=PRECISE)


def chunk_prefixes(transit, inject):
    head_count, chunk_count, key_width = transit.shape[:3]
    value_columns = inject.shape[2]
    maps, injects = transit, inject
    shift = 1
    while shift < chunk_count:
        earlier_maps = jnp.concatenate(
            [
                jnp.broadcast_to(
                    jnp.eye(key_width, dtype=maps.dtype), (head_count, shift, key_width, key_width)
                ),
                maps[:, :-shift],
            ],
            axis=1,
        )
        earlier_injects = jnp.concatenate(
            [
                jnp.zeros((head_count, shift, value_columns, key_width), injects.dtype),
                injects[:, :-shift],
            ],
            axis=1,
        )
        injects = (
            jnp.einsum("hcvk,hckl->hcvl", earlier_injects, maps, precision=PRECISE) + injects
        )
        maps = jnp.einsum("hcjk,hckl->hcjl", earlier_maps, maps, precision=PRECISE)
        shift *= 2
    chunk_maps = jnp.concatenate(
        [
            jnp.broadcast_to(jnp.eye(key_width, dtype=maps.dtype), (head_count, 1, key_width, key_width)),
            maps[:, :-1],
        ],
        axis=1,
    )
    chunk_injects = jnp.concatenate(
        [jnp.zeros((head_count, 1, value_columns, key_width), injects.dtype), injects[:, :-1]],
        axis=1,
    )
    return (maps[:, -1], injects[:, -1]), (chunk_maps, chunk_injects)


def finish(raw_out, norm_gain):
    head_count, span_count, query_count, value_columns = raw_out.shape
    rows_out = raw_out.reshape(head_count, span_count * query_count, value_columns)
    scaled = (
        rows_out
        * lax.rsqrt(jnp.mean(rows_out * rows_out, axis=-1, keepdims=True) + NORM_EPSILON)
        * norm_gain
    )
    return (
        scaled.transpose(1, 0, 2)
        .reshape(span_count * query_count, head_count * value_columns)
        .astype(jnp.bfloat16)
    )


def local(
    queries,
    key_pairs,
    value_pairs,
    beta_pairs,
    log_decay,
    query_filter_taps,
    conv_key,
    conv_value,
    norm_gain,
    out_weight,
):
    piece_list = queries.shape[0]
    rim_start = piece_list - (query_filter_taps.shape[0] - 1)
    rim_queries, rim_keys, rim_values = shifted(
        (queries[rim_start:], key_pairs[rim_start:], value_pairs[rim_start:]), "ctx", 1
    )
    query_hat, local_out, transit, inject = prepare(
        queries,
        key_pairs,
        value_pairs,
        beta_pairs,
        log_decay,
        query_filter_taps,
        conv_key,
        conv_value,
        rim_queries,
        rim_keys,
        rim_values,
    )
    head_count = transit.shape[0]
    key_width = transit.shape[-1]
    value_columns = inject.shape[-2]
    (device_map, device_inject), (chunk_maps, chunk_injects) = chunk_prefixes(transit, inject)
    mapped_queries = jnp.einsum("hctd,hced->hcte", query_hat, chunk_maps, precision=PRECISE)
    known_out = local_out + jnp.einsum(
        "hctd,hcvd->hctv", query_hat, chunk_injects, precision=PRECISE
    )
    ctx_count = lax.axis_size("ctx")
    ctx_index = lax.axis_index("ctx")
    width = 1
    while 2 * width < ctx_count - 1:
        earlier_map, earlier_inject = jnp.split(
            shifted(jnp.concatenate([device_map, device_inject], axis=1), "ctx", width), 2, axis=1
        )
        device_inject = matmul_heads(earlier_inject, device_map) + device_inject
        device_map = jnp.where(
            ctx_index >= width, matmul_heads(earlier_map, device_map), device_map
        )
        width *= 2
    near_map, near_inject = jnp.split(
        shifted(jnp.concatenate([device_map, device_inject], axis=1), "ctx", 1), 2, axis=1
    )
    far_inject = shifted(device_inject, "ctx", width + 1)
    entering = matmul_heads(far_inject, near_map) + near_inject
    raw_out = known_out + jnp.einsum("hcte,hve->hctv", mapped_queries, entering, precision=PRECISE)
    normed = finish(raw_out, norm_gain)
    head_devices = lax.axis_size("head")
    head_index = lax.axis_index("head")
    group_width = normed.shape[1]
    layer_out = None
    for step in range(head_devices):
        if step == 0:
            group_rows = normed
        else:
            group_rows = lax.ppermute(
                normed, "head", [(source, (source + step) % head_devices) for source in range(head_devices)]
            )
        group_weight = lax.dynamic_slice_in_dim(
            out_weight, ((head_index - step) % head_devices) * group_width, group_width, axis=0
        )
        part = jnp.dot(group_rows, group_weight, preferred_element_type=jnp.float32)
        layer_out = part if layer_out is None else layer_out + part
    return layer_out.astype(jnp.bfloat16)


def solution(mesh):
    return jax.shard_map(
        local,
        mesh=mesh,
        in_specs=(
            P("ctx", "head"),
            P("ctx", None, "head"),
            P("ctx", None, "head"),
            P("ctx", None, "head"),
            P("ctx", "head"),
            P(None, "head"),
            P(None, None, "head"),
            P(None, None, "head"),
            P(),
            P(None, "head"),
        ),
        out_specs=P("ctx", "head"),
        check_vma=False,
    )
```
